32 devices in a mesh: row: 4 (over z), col: 8 (over y, x, core).
Axes of the slice: x: 2, y: 2, z: 4, core: 2. Of those that a mesh axis runs over, the one named last changes fastest.
Arguments:
- tokens: bfloat16 [256, 8192], P('col', 'row'), may hold values from -6 to 6
- out_grad: bfloat16 [256, 8192], P('col', 'row'), may hold values from -1.1953125 to 1.1953125
- w_gate: bfloat16 [8192, 16384], P('row', 'col'), may hold values from -0.0625 to 0.0625
- w_up: bfloat16 [8192, 16384], P('row', 'col'), may hold values from -0.0625 to 0.0625
- w_down: bfloat16 [16384, 8192], P('col', 'row'), may hold values from -0.046875 to 0.046875
Outputs:
- grad_input: bfloat16 [256, 8192], P('col', 'row')
- grad_gate: bfloat16 [8192, 16384], P('row', 'col')
- grad_up: bfloat16 [8192, 16384], P('row', 'col')
- grad_down: bfloat16 [16384, 8192], P('col', 'row')
The draws below stay inside these ranges and needn't reach their ends.
All inputs are finite; a program needn't handle non-finite values.
Results may differ from the reference program's by a relative error of at most 0.0049.
Values may be sent and summed in bfloat16 or wider, within the bound.
A program may use at most 128 MiB of HBM per device.

```python
import jax
import jax.numpy as jnp
from jax import lax

D = 8192
FF = 16384
TOKENS = 256


def strengthened(result, stream_key, source, target, shards_of, factor):
    def block_of(dim):
        return (jnp.arange(result.shape[dim]) // (result.shape[dim] // shards_of)).reshape((-1,) + (1,) * (result.ndim - 1 - dim))

    first = jax.random.permutation(stream_key, shards_of)[block_of(target)]
    second = (block_of(target) + shards_of // 2) % shards_of
    return jnp.where((block_of(source) == first) | (block_of(source) == second), factor * result, result)


def shard_levels(stream_key, shape, split, low, largest):
    def one(dim, parts):
        heights = jax.random.uniform(jax.random.fold_in(jax.random.fold_in(stream_key, 6), dim), (parts,), jnp.float32, low / len(split), largest / len(split))
        return jnp.repeat(jnp.exp(heights), shape[dim] // parts).reshape((-1,) + (1,) * (len(shape) - dim - 1))

    level = one(*split[0])
    for cut in split[1:]:
        level = level * one(*cut)
    return level


def gaussian(rng, shape, spread, reach, split=(), kind=jnp.bfloat16):
    gain = shard_levels(rng, shape, split, -0.22, 0.18) if split else 1.0
    drawn = jax.random.normal(rng, shape, jnp.float32) * spread * gain
    return jnp.minimum(jnp.maximum(drawn, -reach), reach).astype(kind)


def bell_draw_with(own_key, shape, spread, reach, shards, heavy, dtype=jnp.bfloat16):
    drawn = spread * jax.random.normal(own_key, shape, jnp.float32)
    if shards:
        drawn = drawn * shard_levels(own_key, shape, shards, -0.22, 0.18)
    return jnp.clip(strengthened(drawn, jax.random.fold_in(own_key, 3), *heavy), -reach, reach).astype(dtype)


def setup_inputs(seed: int = 0) -> dict:
    streams_of = jax.random.split(jax.random.key(seed), 6)
    tokens = bell_draw_with(streams_of[0], (TOKENS, D), 1.0, 6.0, ((0, 8), (1, 4)), (1, 0, 8, 2.0))
    out_grad = bell_draw_with(streams_of[1], (TOKENS, D), 0.2, 1.1953125, ((0, 8), (1, 4)), (1, 0, 8, 2.0))
    w_gate = gaussian(streams_of[2], (D, FF), D ** -0.5, 0.0625, ((0, 4), (1, 8)))
    w_up = gaussian(streams_of[3], (D, FF), D ** -0.5, 0.0625, ((0, 4), (1, 8)))
    w_down = gaussian(streams_of[4], (FF, D), FF ** -0.5, 0.046875, ((0, 8), (1, 4)))
    return dict(tokens=tokens, out_grad=out_grad, w_gate=w_gate, w_up=w_up, w_down=w_down)


def contract(left_array, right_array, left_dim, right_dim):
    return lax.dot_general(left_array, right_array, (((left_dim,), (right_dim,)), ((), ())), preferred_element_type=jnp.float32)


def swiglu_back(gate_sum, up_sum, hidden_grad):
    logistic = jax.nn.sigmoid(gate_sum)
    active = gate_sum * logistic
    hidden = (active * up_sum).astype(jnp.bfloat16)
    up_grad = (hidden_grad * active).astype(jnp.bfloat16)
    gate_grad = (hidden_grad * up_sum * logistic * (1.0 + gate_sum * (1.0 - logistic))).astype(jnp.bfloat16)
    return hidden, gate_grad, up_grad


def reference(tokens, out_grad, w_gate, w_up, w_down):
    gate_sum = jnp.dot(tokens, w_gate, preferred_element_type=jnp.float32)
    up_sum = jnp.dot(tokens, w_up, preferred_element_type=jnp.float32)
    hidden_grad = contract(out_grad, w_down, 1, 1)
    hidden, gate_grad, up_grad = swiglu_back(gate_sum, up_sum, hidden_grad)
    grad_down = contract(hidden, out_grad, 0, 0).astype(jnp.bfloat16)
    grad_gate = contract(tokens, gate_grad, 0, 0).astype(jnp.bfloat16)
    grad_up = contract(tokens, up_grad, 0, 0).astype(jnp.bfloat16)
    grad_input = (contract(gate_grad, w_gate, 1, 1) + contract(up_grad, w_up, 1, 1)).astype(jnp.bfloat16)
    return grad_input, grad_gate, grad_up, grad_down
```

```python
import jax
import jax.numpy as jnp
from jax import lax
from jax.experimental import pallas as pl
from jax.experimental.pallas import tpu as pltpu
from jax.sharding import PartitionSpec as P

BF16 = jnp.bfloat16
F32 = jnp.float32


def contract(left_array, right_array, left_dim, right_dim):
    return lax.dot_general(
        left_array,
        right_array,
        (((left_dim,), (right_dim,)), ((), ())),
        preferred_element_type=F32,
    )


def swiglu_back(gate_sum, up_sum, hidden_grad):
    logistic = jax.nn.sigmoid(gate_sum)
    active = gate_sum * logistic
    hidden = (active * up_sum).astype(BF16)
    up_grad = (hidden_grad * active).astype(BF16)
    gate_grad = (hidden_grad * up_sum * logistic * (1.0 + gate_sum * (1.0 - logistic))).astype(BF16)
    return (hidden, gate_grad, up_grad)


def weight_grads_kernel(xt, ht, gg, ug, og, out_gate, out_up, out_down):
    out_gate[...] = jnp.dot(xt[...], gg[...], preferred_element_type=F32).astype(BF16)
    out_up[...] = jnp.dot(xt[...], ug[...], preferred_element_type=F32).astype(BF16)
    out_down[...] = jnp.dot(ht[...], og[...], preferred_element_type=F32).astype(BF16)


def weight_grads(tokens_t, hidden_t, gate_grad, up_grad, all_grads):
    d, t = tokens_t.shape
    f = hidden_t.shape[0]
    steps = 8
    whole = lambda a: pl.BlockSpec(a.shape, lambda i: (0, 0))
    return pl.pallas_call(
        weight_grads_kernel,
        grid=(steps,),
        in_specs=[
            pl.BlockSpec((d // steps, t), lambda i: (i, 0)),
            pl.BlockSpec((f // steps, t), lambda i: (i, 0)),
            whole(gate_grad),
            whole(up_grad),
            whole(all_grads),
        ],
        out_specs=[
            pl.BlockSpec((d // steps, f), lambda i: (i, 0)),
            pl.BlockSpec((d // steps, f), lambda i: (i, 0)),
            pl.BlockSpec((f // steps, d), lambda i: (i, 0)),
        ],
        out_shape=[
            jax.ShapeDtypeStruct((d, f), BF16),
            jax.ShapeDtypeStruct((d, f), BF16),
            jax.ShapeDtypeStruct((f, d), BF16),
        ],
        compiler_params=pltpu.CompilerParams(vmem_limit_bytes=40 * 2**20),
        cost_estimate=pl.CostEstimate(
            flops=6 * t * d * f, bytes_accessed=6 * d * f + 10 * t * d, transcendentals=0
        ),
    )(tokens_t, hidden_t, gate_grad, up_grad, all_grads)


def shards(tokens, out_grad, w_gate, w_up, w_down):
    all_tokens = lax.all_gather(tokens, "col", axis=0, tiled=True)
    all_grads = lax.all_gather(out_grad, "col", axis=0, tiled=True)
    gate_part = jnp.dot(all_tokens, w_gate, preferred_element_type=F32)
    up_part = jnp.dot(all_tokens, w_up, preferred_element_type=F32)
    grad_part = contract(all_grads, w_down, 1, 1)
    scattered = [
        lax.psum_scatter(p, "row", scatter_dimension=0, tiled=True)
        for p in (gate_part, up_part, grad_part)
    ]
    hidden, gate_grad, up_grad = [
        lax.all_gather(v, "row", axis=0, tiled=True) for v in swiglu_back(*scattered)
    ]
    share = contract(gate_grad, w_gate, 1, 1) + contract(up_grad, w_up, 1, 1)
    grad_input = lax.psum_scatter(share, "col", scatter_dimension=0, tiled=True).astype(BF16)
    grad_gate, grad_up, grad_down = weight_grads(
        all_tokens.T, hidden.T, gate_grad, up_grad, all_grads
    )
    return (grad_input, grad_gate, grad_up, grad_down)


def solution(mesh):
    return jax.shard_map(
        shards,
        mesh=mesh,
        in_specs=(
            P("col", "row"),
            P("col", "row"),
            P("row", "col"),
            P("row", "col"),
            P("col", "row"),
        ),
        out_specs=(P("col", "row"), P("row", "col"), P("row", "col"), P("col", "row")),
        check_vma=False,
    )
```

```python
import functools

import jax
import jax.numpy as jnp
from jax import lax
from jax.experimental import pallas as pl
from jax.experimental.pallas import tpu as pltpu
from jax.sharding import PartitionSpec as P

BF16 = jnp.bfloat16
F32 = jnp.float32


def contract(left_array, right_array, left_dim, right_dim):
    return lax.dot_general(
        left_array,
        right_array,
        (((left_dim,), (right_dim,)), ((), ())),
        preferred_element_type=F32,
    )


def swiglu_back(gate_sum, up_sum, hidden_grad):
    logistic = jax.nn.sigmoid(gate_sum)
    active = gate_sum * logistic
    hidden = (active * up_sum).astype(BF16)
    up_grad = (hidden_grad * active).astype(BF16)
    gate_grad = (hidden_grad * up_sum * logistic * (1.0 + gate_sum * (1.0 - logistic))).astype(BF16)
    return (hidden, gate_grad, up_grad)


def forward_kernel(
    n, ncol, cw, tbs, lag,
    x_ref, g_ref, wg_hbm, wu_hbm, wd_hbm,
    xa, ga, out,
    wg, wu, wd, part, sent, got,
    w_sem, own_sem, ag_send, ag_recv, re_send, re_recv, up_send, up_recv, dn_send, dn_recv,
):
    row, col = lax.axis_index("row"), lax.axis_index("col")
    tl = x_ref.shape[0]
    t, f = out.shape[1], out.shape[2]
    per_half = f // 2 // cw
    tb = t // tbs
    chunks = per_half * tb
    peers = ncol // 2
    core = lax.rem(col, 2)
    sibling = col + 1 - 2 * core
    mesh_id = pl.DeviceIdType.MESH

    def weight_copies(b):
        cols = pl.ds(pl.multiple_of(b * cw, cw), cw)
        return (
            pltpu.make_async_copy(wg_hbm.at[:, cols], wg.at[:, cols], w_sem.at[0, b]),
            pltpu.make_async_copy(wu_hbm.at[:, cols], wu.at[:, cols], w_sem.at[1, b]),
            pltpu.make_async_copy(wd_hbm.at[cols, :], wd.at[cols, :], w_sem.at[2, b]),
        )

    for c in range(per_half):
        for b in (c, per_half + c):
            for copy in weight_copies(b):
                copy.start()

    def peer(j):
        return lax.rem(col + 2 * j, ncol)

    def rows_of(device):
        return pl.ds(pl.multiple_of(device * tl, tl), tl)

    barrier = pltpu.get_barrier_semaphore()
    pl.semaphore_signal(barrier, inc=1, device_id=(row, sibling), device_id_type=mesh_id)
    for j in range(1, peers):
        pl.semaphore_signal(barrier, inc=1, device_id=(row, peer(j)), device_id_type=mesh_id)

    for near in (lax.rem(row + 1, n), lax.rem(row + n - 1, n)):
        pl.semaphore_signal(barrier, inc=1, device_id=(near, col), device_id_type=mesh_id)
    pl.semaphore_wait(barrier, peers + 2)

    def first_copy(a, j):
        src, dst = ((x_ref, xa), (g_ref, ga))[a]
        return pltpu.make_async_remote_copy(
            src_ref=src,
            dst_ref=dst.at[rows_of(col), :],
            send_sem=ag_send.at[a, j],
            recv_sem=ag_recv.at[a, j],
            device_id=(row, sibling if j == 0 else peer(j)),
            device_id_type=mesh_id,
        )

    def relay_copy(a, j):
        dst = (xa, ga)[a]
        block = dst.at[rows_of(lax.rem(col + ncol - 2 * j, ncol)), :]
        return pltpu.make_async_remote_copy(
            src_ref=block,
            dst_ref=block,
            send_sem=re_send.at[a, j],
            recv_sem=re_recv.at[a, j],
            device_id=(row, sibling),
            device_id_type=mesh_id,
        )

    own = [
        pltpu.make_async_copy(src, dst.at[rows_of(col), :], own_sem.at[a])
        for a, (src, dst) in enumerate(((x_ref, xa), (g_ref, ga)))
    ]
    for a in range(2):
        for j in range(1, peers):
            first_copy(a, j).start()
        first_copy(a, 0).start()
        own[a].start()
    for a in range(2):
        for j in range(1, peers):
            first_copy(a, j).wait_recv()
            relay_copy(a, j).start()
    for a in range(2):
        own[a].wait()
        first_copy(a, 0).wait_recv()
        for j in range(1, peers):
            relay_copy(a, j).wait_recv()

    places = (row, n - 1 - row)
    ups = (row + 1, row - 1)
    downs = (row - 1, row + 1)

    def spot(h, k):
        b = h * per_half + k // tb
        r = pl.ds(pl.multiple_of(lax.rem(k, tb) * tbs, tbs), tbs)
        return b, r, pl.ds(pl.multiple_of(b * cw, cw), cw)

    def up_copy(h, k):
        return pltpu.make_async_remote_copy(
            src_ref=sent.at[h, k],
            dst_ref=got.at[h, k],
            send_sem=up_send.at[h, k],
            recv_sem=up_recv.at[h, k],
            device_id=(ups[h], col),
            device_id_type=mesh_id,
        )

    def down_copy(h, k):
        _, r, c = spot(h, k)
        return pltpu.make_async_remote_copy(
            src_ref=out.at[:, r, c],
            dst_ref=out.at[:, r, c],
            send_sem=dn_send.at[h, k],
            recv_sem=dn_recv.at[h, k],
            device_id=(downs[h], col),
            device_id_type=mesh_id,
        )

    def reduce_chunk(h, k):
        place = places[h]
        b, r, c = spot(h, k)

        @pl.when(place > 0)
        def _():
            up_copy(h, k).wait_recv()
            for i in range(3):
                part[b, i, r, :] += got[h, k, i].astype(F32)

        @pl.when(place < n - 1)
        def _():
            for i in range(3):
                sent[h, k, i] = part[b, i, r, :].astype(BF16)
            up_copy(h, k).start()

        @pl.when(place == n - 1)
        def _():
            values = swiglu_back(part[b, 0, r, :], part[b, 1, r, :], part[b, 2, r, :])
            for i in range(3):
                out[i, r, c] = values[i]
            down_copy(h, k).start()

    def step(s, carry):
        @pl.when((s < chunks) & (lax.rem(s, tb) == 0))
        def _():
            for h in range(2):
                b = h * per_half + s // tb
                for copy in weight_copies(b):
                    copy.wait()
                cols = pl.ds(pl.multiple_of(b * cw, cw), cw)
                part[b, 0] = jnp.dot(xa[...], wg[:, cols], preferred_element_type=F32)
                part[b, 1] = jnp.dot(xa[...], wu[:, cols], preferred_element_type=F32)
                part[b, 2] = contract(ga[...], wd[cols, :], 1, 1)

        for h in range(2):
            k = s - lag * places[h]

            @pl.when((k >= 0) & (k < chunks))
            def _():
                reduce_chunk(h, k)

        for h in range(2):
            k = s - lag * (2 * (n - 1) - places[h])

            @pl.when((k >= 0) & (k < chunks) & (places[h] < n - 1))
            def _():
                down_copy(h, k).wait_recv()

                @pl.when(places[h] > 0)
                def _():
                    down_copy(h, k).start()

        return carry

    lax.fori_loop(0, chunks + 2 * lag * (n - 1), step, 0)

    for a in range(2):
        for j in range(peers):
            first_copy(a, j).wait_send()
            if j:
                relay_copy(a, j).wait_send()

    def drain(k, carry):
        for h in range(2):

            @pl.when(places[h] < n - 1)
            def _():
                up_copy(h, k).wait_send()

            @pl.when(places[h] > 0)
            def _():
                down_copy(h, k).wait_send()

        return carry

    lax.fori_loop(0, chunks, drain, 0)


def forward(n, ncol, tokens, out_grad, w_gate, w_up, w_down):
    tl, d = tokens.shape
    f = w_gate.shape[1]
    t = tl * ncol
    cw = min(256, f // 2)
    tbs, lag = 64, 2
    chunks = f // 2 // cw * (t // tbs)
    blocks = f // cw
    vmem = pl.BlockSpec(memory_space=pltpu.VMEM)
    hbm = pl.BlockSpec(memory_space=pl.ANY)
    dma = pltpu.SemaphoreType.DMA
    return pl.pallas_call(
        functools.partial(forward_kernel, n, ncol, cw, tbs, lag),
        out_shape=[
            jax.ShapeDtypeStruct((t, d), BF16),
            jax.ShapeDtypeStruct((t, d), BF16),
            jax.ShapeDtypeStruct((3, t, f), BF16),
        ],
        in_specs=[vmem, vmem, hbm, hbm, hbm],
        out_specs=[vmem, vmem, vmem],
        scratch_shapes=[
            pltpu.VMEM((d, f), BF16),
            pltpu.VMEM((d, f), BF16),
            pltpu.VMEM((f, d), BF16),
            pltpu.VMEM((blocks, 3, t, cw), F32),
            pltpu.VMEM((2, chunks, 3, tbs, cw), BF16),
            pltpu.VMEM((2, chunks, 3, tbs, cw), BF16),
            dma((3, blocks)),
            dma((2,)),
            dma((2, ncol // 2)),
            dma((2, ncol // 2)),
            dma((2, ncol // 2)),
            dma((2, ncol // 2)),
            dma((2, chunks)),
            dma((2, chunks)),
            dma((2, chunks)),
            dma((2, chunks)),
        ],
        compiler_params=pltpu.CompilerParams(
            collective_id=0, has_side_effects=True, vmem_limit_bytes=58 * 2**20
        ),
    )(tokens, out_grad, w_gate, w_up, w_down)


def weight_grads_kernel(xt, ht, gg, ug, og, out_gate, out_up, out_down):
    out_gate[...] = jnp.dot(xt[...], gg[...], preferred_element_type=F32).astype(BF16)
    out_up[...] = jnp.dot(xt[...], ug[...], preferred_element_type=F32).astype(BF16)
    out_down[...] = jnp.dot(ht[...], og[...], preferred_element_type=F32).astype(BF16)


def weight_grads(tokens_t, hidden_t, gate_grad, up_grad, all_grads):
    d, t = tokens_t.shape
    f = hidden_t.shape[0]
    steps = 8
    whole = lambda a: pl.BlockSpec(a.shape, lambda i: (0, 0))
    return pl.pallas_call(
        weight_grads_kernel,
        grid=(steps,),
        in_specs=[
            pl.BlockSpec((d // steps, t), lambda i: (i, 0)),
            pl.BlockSpec((f // steps, t), lambda i: (i, 0)),
            whole(gate_grad),
            whole(up_grad),
            whole(all_grads),
        ],
        out_specs=[
            pl.BlockSpec((d // steps, f), lambda i: (i, 0)),
            pl.BlockSpec((d // steps, f), lambda i: (i, 0)),
            pl.BlockSpec((f // steps, d), lambda i: (i, 0)),
        ],
        out_shape=[
            jax.ShapeDtypeStruct((d, f), BF16),
            jax.ShapeDtypeStruct((d, f), BF16),
            jax.ShapeDtypeStruct((f, d), BF16),
        ],
        compiler_params=pltpu.CompilerParams(vmem_limit_bytes=40 * 2**20),
        cost_estimate=pl.CostEstimate(
            flops=6 * t * d * f, bytes_accessed=6 * d * f + 10 * t * d, transcendentals=0
        ),
    )(tokens_t, hidden_t, gate_grad, up_grad, all_grads)


def shards(n, ncol, tokens, out_grad, w_gate, w_up, w_down):
    all_tokens, all_grads, results = forward(n, ncol, tokens, out_grad, w_gate, w_up, w_down)
    hidden, gate_grad, up_grad = results[0], results[1], results[2]
    share = contract(gate_grad, w_gate, 1, 1) + contract(up_grad, w_up, 1, 1)
    grad_input = lax.psum_scatter(share, "col", scatter_dimension=0, tiled=True).astype(BF16)
    grad_gate, grad_up, grad_down = weight_grads(
        all_tokens.T, hidden.T, gate_grad, up_grad, all_grads
    )
    return (grad_input, grad_gate, grad_up, grad_down)


def solution(mesh):
    return jax.shard_map(
        functools.partial(shards, mesh.shape["row"], mesh.shape["col"]),
        mesh=mesh,
        in_specs=(
            P("col", "row"),
            P("col", "row"),
            P("row", "col"),
            P("row", "col"),
            P("col", "row"),
        ),
        out_specs=(P("col", "row"), P("row", "col"), P("row", "col"), P("col", "row")),
        check_vma=False,
    )
```

```python
import functools

import jax
import jax.numpy as jnp
from jax import lax
from jax.experimental import pallas as pl
from jax.experimental.pallas import tpu as pltpu
from jax.sharding import PartitionSpec as P

BF16 = jnp.bfloat16
F32 = jnp.float32


def contract(left_array, right_array, left_dim, right_dim):
    return lax.dot_general(
        left_array,
        right_array,
        (((left_dim,), (right_dim,)), ((), ())),
        preferred_element_type=F32,
    )


def swiglu_back(gate_sum, up_sum, hidden_grad):
    logistic = jax.nn.sigmoid(gate_sum)
    active = gate_sum * logistic
    hidden = (active * up_sum).astype(BF16)
    up_grad = (hidden_grad * active).astype(BF16)
    gate_grad = (hidden_grad * up_sum * logistic * (1.0 + gate_sum * (1.0 - logistic))).astype(BF16)
    return (hidden, gate_grad, up_grad)


def forward_kernel(
    n, ncol, cw, tbs, lag,
    x_ref, g_ref, wg_hbm, wu_hbm, wd_hbm,
    xa, ga, out,
    wg, wu, wd, part, sent, got,
    w_sem, own_sem, ag_send, ag_recv, re_send, re_recv, up_send, up_recv, dn_send, dn_recv,
):
    row, col = lax.axis_index("row"), lax.axis_index("col")
    tl = x_ref.shape[0]
    t, f = out.shape[1], out.shape[2]
    per_half = f // 2 // cw
    tb = t // tbs
    chunks = per_half * tb
    peers = ncol // 2
    core = lax.rem(col, 2)
    sibling = col + 1 - 2 * core
    mesh_id = pl.DeviceIdType.MESH

    def weight_copies(b):
        cols = pl.ds(pl.multiple_of(b * cw, cw), cw)
        return (
            pltpu.make_async_copy(wg_hbm.at[:, cols], wg.at[:, cols], w_sem.at[0, b]),
            pltpu.make_async_copy(wu_hbm.at[:, cols], wu.at[:, cols], w_sem.at[1, b]),
            pltpu.make_async_copy(wd_hbm.at[cols, :], wd.at[cols, :], w_sem.at[2, b]),
        )

    for c in range(per_half):
        for b in (c, per_half + c):
            for copy in weight_copies(b):
                copy.start()

    def peer(j):
        return lax.rem(col + 2 * j, ncol)

    def rows_of(device):
        return pl.ds(pl.multiple_of(device * tl, tl), tl)

    barrier = pltpu.get_barrier_semaphore()
    pl.semaphore_signal(barrier, inc=1, device_id=(row, sibling), device_id_type=mesh_id)
    for j in range(1, peers):
        pl.semaphore_signal(barrier, inc=1, device_id=(row, peer(j)), device_id_type=mesh_id)

    for near in (lax.rem(row + 1, n), lax.rem(row + n - 1, n)):
        pl.semaphore_signal(barrier, inc=1, device_id=(near, col), device_id_type=mesh_id)
    pl.semaphore_wait(barrier, peers + 2)

    def first_copy(a, j):
        src, dst = ((x_ref, xa), (g_ref, ga))[a]
        return pltpu.make_async_remote_copy(
            src_ref=src,
            dst_ref=dst.at[rows_of(col), :],
            send_sem=ag_send.at[a, j],
            recv_sem=ag_recv.at[a, j],
            device_id=(row, sibling if j == 0 else peer(j)),
            device_id_type=mesh_id,
        )

    def relay_copy(a, j):
        dst = (xa, ga)[a]
        block = dst.at[rows_of(lax.rem(col + ncol - 2 * j, ncol)), :]
        return pltpu.make_async_remote_copy(
            src_ref=block,
            dst_ref=block,
            send_sem=re_send.at[a, j],
            recv_sem=re_recv.at[a, j],
            device_id=(row, sibling),
            device_id_type=mesh_id,
        )

    own = [
        pltpu.make_async_copy(src, dst.at[rows_of(col), :], own_sem.at[a])
        for a, (src, dst) in enumerate(((x_ref, xa), (g_ref, ga)))
    ]
    for a in range(2):
        for j in range(1, peers):
            first_copy(a, j).start()
        first_copy(a, 0).start()
        own[a].start()
    for a in range(2):
        for j in range(1, peers):
            first_copy(a, j).wait_recv()
            relay_copy(a, j).start()
    for a in range(2):
        own[a].wait()
        first_copy(a, 0).wait_recv()
        for j in range(1, peers):
            relay_copy(a, j).wait_recv()

    places = (row, n - 1 - row)
    ups = (row + 1, row - 1)
    downs = (row - 1, row + 1)

    def spot(h, k):
        b = h * per_half + k // tb
        r = pl.ds(pl.multiple_of(lax.rem(k, tb) * tbs, tbs), tbs)
        return b, r, pl.ds(pl.multiple_of(b * cw, cw), cw)

    root = n // 2
    away = [jnp.where(place > root, place - root, root - place) for place in places]

    def up_copy(h, k, side):
        return pltpu.make_async_remote_copy(
            src_ref=sent.at[h, k],
            dst_ref=got.at[side, h, k],
            send_sem=up_send.at[side, h, k],
            recv_sem=up_recv.at[side, h, k],
            device_id=((ups, downs)[side][h], col),
            device_id_type=mesh_id,
        )

    def down_copy(h, k, side):
        _, r, c = spot(h, k)
        return pltpu.make_async_remote_copy(
            src_ref=out.at[:, r, c],
            dst_ref=out.at[:, r, c],
            send_sem=dn_send.at[side, h, k],
            recv_sem=dn_recv.at[side, h, k],
            device_id=((downs, ups)[side][h], col),
            device_id_type=mesh_id,
        )

    def reduce_chunk(h, k):
        place = places[h]
        b, r, c = spot(h, k)

        for side, inner in enumerate(
            ((place > 0) & (place <= root), (place >= root) & (place < n - 1))
        ):

            @pl.when(inner)
            def _(side=side):
                up_copy(h, k, side).wait_recv()
                for i in range(3):
                    part[b, i, r, :] += got[side, h, k, i].astype(F32)

        for side, outer in enumerate((place < root, place > root)):

            @pl.when(outer)
            def _(side=side):
                for i in range(3):
                    sent[h, k, i] = part[b, i, r, :].astype(BF16)
                up_copy(h, k, side).start()

        @pl.when(place == root)
        def _():
            values = swiglu_back(part[b, 0, r, :], part[b, 1, r, :], part[b, 2, r, :])
            for i in range(3):
                out[i, r, c] = values[i]
            down_copy(h, k, 0).start()
            down_copy(h, k, 1).start()

    def step(s, carry):
        @pl.when((s < chunks) & (lax.rem(s, tb) == 0))
        def _():
            for h in range(2):
                b = h * per_half + s // tb
                for copy in weight_copies(b):
                    copy.wait()
                cols = pl.ds(pl.multiple_of(b * cw, cw), cw)
                part[b, 0] = jnp.dot(xa[...], wg[:, cols], preferred_element_type=F32)
                part[b, 1] = jnp.dot(xa[...], wu[:, cols], preferred_element_type=F32)
                part[b, 2] = contract(ga[...], wd[cols, :], 1, 1)

        for h in range(2):
            k = s - lag * (root - away[h])

            @pl.when((k >= 0) & (k < chunks))
            def _():
                reduce_chunk(h, k)

        for h in range(2):
            k = s - lag * (root + away[h])
            place = places[h]
            for side, outer, inner in (
                (0, place < root, place > 0),
                (1, place > root, place < n - 1),
            ):

                @pl.when((k >= 0) & (k < chunks) & outer)
                def _(h=h, k=k, side=side, inner=inner):
                    down_copy(h, k, side).wait_recv()

                    @pl.when(inner)
                    def _():
                        down_copy(h, k, side).start()

        return carry

    lax.fori_loop(0, chunks + 2 * lag * root, step, 0)

    for a in range(2):
        for j in range(peers):
            first_copy(a, j).wait_send()
            if j:
                relay_copy(a, j).wait_send()

    def drain(k, carry):
        for h in range(2):
            place = places[h]
            for side, outer, inner in (
                (0, place < root, (place <= root) & (place > 0)),
                (1, place > root, (place >= root) & (place < n - 1)),
            ):

                @pl.when(outer)
                def _(h=h, side=side):
                    up_copy(h, k, side).wait_send()

                @pl.when(inner)
                def _(h=h, side=side):
                    down_copy(h, k, side).wait_send()

        return carry

    lax.fori_loop(0, chunks, drain, 0)


def forward(n, ncol, tokens, out_grad, w_gate, w_up, w_down):
    tl, d = tokens.shape
    f = w_gate.shape[1]
    t = tl * ncol
    cw = min(256, f // 2)
    tbs, lag = 64, 2
    chunks = f // 2 // cw * (t // tbs)
    blocks = f // cw
    vmem = pl.BlockSpec(memory_space=pltpu.VMEM)
    hbm = pl.BlockSpec(memory_space=pl.ANY)
    dma = pltpu.SemaphoreType.DMA
    return pl.pallas_call(
        functools.partial(forward_kernel, n, ncol, cw, tbs, lag),
        out_shape=[
            jax.ShapeDtypeStruct((t, d), BF16),
            jax.ShapeDtypeStruct((t, d), BF16),
            jax.ShapeDtypeStruct((3, t, f), BF16),
        ],
        in_specs=[vmem, vmem, hbm, hbm, hbm],
        out_specs=[vmem, vmem, vmem],
        scratch_shapes=[
            pltpu.VMEM((d, f), BF16),
            pltpu.VMEM((d, f), BF16),
            pltpu.VMEM((f, d), BF16),
            pltpu.VMEM((blocks, 3, t, cw), F32),
            pltpu.VMEM((2, chunks, 3, tbs, cw), BF16),
            pltpu.VMEM((2, 2, chunks, 3, tbs, cw), BF16),
            dma((3, blocks)),
            dma((2,)),
            dma((2, ncol // 2)),
            dma((2, ncol // 2)),
            dma((2, ncol // 2)),
            dma((2, ncol // 2)),
            dma((2, 2, chunks)),
            dma((2, 2, chunks)),
            dma((2, 2, chunks)),
            dma((2, 2, chunks)),
        ],
        compiler_params=pltpu.CompilerParams(
            collective_id=0, has_side_effects=True, vmem_limit_bytes=58 * 2**20
        ),
    )(tokens, out_grad, w_gate, w_up, w_down)


def weight_grads_kernel(xt, ht, gg, ug, og, out_gate, out_up, out_down):
    out_gate[...] = jnp.dot(xt[...], gg[...], preferred_element_type=F32).astype(BF16)
    out_up[...] = jnp.dot(xt[...], ug[...], preferred_element_type=F32).astype(BF16)
    out_down[...] = jnp.dot(ht[...], og[...], preferred_element_type=F32).astype(BF16)


def weight_grads(tokens_t, hidden_t, gate_grad, up_grad, all_grads):
    d, t = tokens_t.shape
    f = hidden_t.shape[0]
    steps = 8
    whole = lambda a: pl.BlockSpec(a.shape, lambda i: (0, 0))
    return pl.pallas_call(
        weight_grads_kernel,
        grid=(steps,),
        in_specs=[
            pl.BlockSpec((d // steps, t), lambda i: (i, 0)),
            pl.BlockSpec((f // steps, t), lambda i: (i, 0)),
            whole(gate_grad),
            whole(up_grad),
            whole(all_grads),
        ],
        out_specs=[
            pl.BlockSpec((d // steps, f), lambda i: (i, 0)),
            pl.BlockSpec((d // steps, f), lambda i: (i, 0)),
            pl.BlockSpec((f // steps, d), lambda i: (i, 0)),
        ],
        out_shape=[
            jax.ShapeDtypeStruct((d, f), BF16),
            jax.ShapeDtypeStruct((d, f), BF16),
            jax.ShapeDtypeStruct((f, d), BF16),
        ],
        compiler_params=pltpu.CompilerParams(vmem_limit_bytes=40 * 2**20),
        cost_estimate=pl.CostEstimate(
            flops=6 * t * d * f, bytes_accessed=6 * d * f + 10 * t * d, transcendentals=0
        ),
    )(tokens_t, hidden_t, gate_grad, up_grad, all_grads)


def shards(n, ncol, tokens, out_grad, w_gate, w_up, w_down):
    all_tokens, all_grads, results = forward(n, ncol, tokens, out_grad, w_gate, w_up, w_down)
    hidden, gate_grad, up_grad = results[0], results[1], results[2]
    share = contract(gate_grad, w_gate, 1, 1) + contract(up_grad, w_up, 1, 1)
    grad_input = lax.psum_scatter(share, "col", scatter_dimension=0, tiled=True).astype(BF16)
    grad_gate, grad_up, grad_down = weight_grads(
        all_tokens.T, hidden.T, gate_grad, up_grad, all_grads
    )
    return (grad_input, grad_gate, grad_up, grad_down)


def solution(mesh):
    return jax.shard_map(
        functools.partial(shards, mesh.shape["row"], mesh.shape["col"]),
        mesh=mesh,
        in_specs=(
            P("col", "row"),
            P("col", "row"),
            P("row", "col"),
            P("row", "col"),
            P("col", "row"),
        ),
        out_specs=(P("col", "row"), P("row", "col"), P("row", "col"), P("col", "row")),
        check_vma=False,
    )
```
